32 devices in a mesh: lb: 8 (over y, x, core), rb: 4 (over z).
Axes of the slice: x: 2, y: 2, z: 4, core: 2. Of those that a mesh axis runs over, the one named last changes fastest.
Arguments:
- wavefunction: bfloat16 [3072, 4, 3072], P('lb', None, 'rb'), may hold values from -6 to 6
- left_environment: bfloat16 [8, 1024, 3072], P(None, 'lb'), may hold values from -0.109375 to 0.109375
- operator_left: float32 [8, 8, 2, 2], replicated, may hold values from -1.5 to 1.5
- operator_right: float32 [8, 8, 2, 2], replicated, may hold values from -1.5 to 1.5
- right_environment: bfloat16 [8, 3072, 3072], P(None, 'rb', 'lb'), may hold values from -0.0546875 to 0.0546875
- row_sector: int32 [8], replicated, may hold values from 0 to 3, never falling along the last dimension, each value on 1 to 4 neighbouring positions
Outputs:
- applied_state: bfloat16 [1024, 4, 3072], P('lb', None, 'rb')
- density: float32 [1024, 1024], P('lb', 'rb')
The draws below stay inside these ranges and needn't reach their ends.
Inputs may be any that keep to these rules, and one draw needn't show every extreme that they name: `row_sector`: entry t is the sector of output rows t * 128 to (t + 1) * 128 - 1. Entries never fall along t; each sector holds 1 to 4 tiles, and one holds exactly 4.
All inputs are finite; a program needn't handle non-finite values.
Results may differ from the reference program's by a relative error of at most 0.013.
Values may be sent and summed in bfloat16 or wider, within the bound.
No kernel may reach another device: no remote copies, remote signals or barrier semaphores. Data moves between devices by JAX's collectives and lax.ppermute only.
A program may use at most 128 MiB of HBM per device.

```python
import math
import jax
import jax.numpy as jnp
import numpy as np
from jax import lax

BOND_WIDTH = 3072
CHANNELS = 8
ROW_DEV = 128
SECTOR_TILES = 4
TILES = 8
ROWS = 1024
SECTORS = 4


def raised(values, rng, source, target, blocks, factor):
    owner, partner = [(jnp.arange(values.shape[position]) // (values.shape[position] // blocks)).reshape([-1 if axis == position else 1 for axis in range(values.ndim)]) for position in (source, target)]
    chosen = jax.random.permutation(rng, blocks)[partner]
    strong = (owner == chosen) | (owner == (partner + blocks // 2) % blocks)
    return jnp.where(strong, factor * values, values)


def steps_of(key, dims, cuts, least, high):
    factor_of, own = 1.0, jax.random.fold_in(key, 6)
    for axis_at, shards_of in cuts:
        heights = jnp.exp(jax.random.uniform(jax.random.fold_in(own, axis_at), (shards_of,), jnp.float32, least / len(cuts), high / len(cuts)))
        factor_of = factor_of * jnp.repeat(heights, dims[axis_at] // shards_of).reshape([-1 if axis == axis_at else 1 for axis in range(len(dims))])
    return factor_of


def profile(number_of, total, reach, lean):
    portions = [(1 << 20) // math.isqrt(standing ** lean) + 1 for standing in range(2, number_of + 1)]
    rest, given = total - reach - (number_of - 1), [1] * (number_of - 1)
    while rest > 0:
        candidates = [i for i in range(number_of - 1) if given[i] < reach]
        whole, left = sum([portions[i] for i in candidates]), rest
        for i in candidates:
            more = min(reach - given[i], max(1, left * portions[i] // whole), rest)
            given[i] = given[i] + more
            rest = rest - more
    return np.array([reach] + given)


def uneven_parts(key, number_of, total, most, lean):
    if number_of == 2:
        one = jax.random.randint(key, (), max(1, total - most), min(most, total - 1) + 1)
        return jnp.stack([one, total - one])
    tallies = jnp.asarray(profile(number_of, total, most, lean), jnp.int32)
    couples = (number_of - 1) // 2
    source_of, taker = tallies[1:1 + 2 * couples:2], tallies[2:2 + 2 * couples:2]
    margin = jnp.minimum(source_of - 1, most - taker)
    passed = jax.random.randint(jax.random.fold_in(key, 1), (couples,), 0, 1 << 20) % (margin + 1)
    tallies = tallies.at[1:1 + 2 * couples:2].set(source_of - passed).at[2:2 + 2 * couples:2].set(taker + passed)
    return tallies[jax.random.permutation(jax.random.fold_in(key, 2), number_of)]


def centred(stream_key, dims, deviation, limit, split=(), dtype=jnp.bfloat16):
    factor_of = steps_of(stream_key, dims, split, -0.22, 0.18) if split else 1.0
    drawn = jax.random.normal(stream_key, dims, jnp.float32) * deviation * factor_of
    return jnp.minimum(jnp.maximum(drawn, -limit), limit).astype(dtype)


def bell_draw_with(stream_key, shape, width, reach, shards, heavy, held_as=jnp.bfloat16):
    entries = width * jax.random.normal(stream_key, shape, jnp.float32)
    if shards:
        entries = entries * steps_of(stream_key, shape, shards, -0.22, 0.18)
    return jnp.clip(raised(entries, jax.random.fold_in(stream_key, 3), *heavy), -reach, reach).astype(held_as)


def setup_inputs(seed: int = 0) -> dict:
    streams_of = jax.random.split(jax.random.key(seed), 7)
    wavefunction = centred(streams_of[0], (BOND_WIDTH, 4, BOND_WIDTH), 1.0, 6.0, ((0, 8), (2, 4)))
    left_environment = centred(streams_of[1], (CHANNELS, ROWS, BOND_WIDTH), BOND_WIDTH ** -0.5, 0.109375, ((1, 8),))
    operator_left = centred(streams_of[2], (CHANNELS, CHANNELS, 2, 2), (2 * CHANNELS) ** -0.5, 1.5, (), jnp.float32)
    operator_right = centred(streams_of[3], (CHANNELS, CHANNELS, 2, 2), (2 * CHANNELS) ** -0.5, 1.5, (), jnp.float32)
    right_environment = bell_draw_with(streams_of[4], (CHANNELS, BOND_WIDTH, BOND_WIDTH), (CHANNELS * BOND_WIDTH) ** -0.5, 0.0546875, ((1, 4), (2, 8)), (1, 2, 8, 2.0))
    row_sector = jnp.searchsorted(jnp.cumsum(uneven_parts(streams_of[5], SECTORS, TILES, SECTOR_TILES, 0)), jnp.arange(TILES), side="right").astype(jnp.int32)
    return dict(wavefunction=wavefunction, left_environment=left_environment, operator_left=operator_left, operator_right=operator_right, right_environment=right_environment, row_sector=row_sector)


def combine_operators(operator_left, operator_right):
    channels = operator_left.shape[0]
    joined = jnp.einsum('aups,uvqt->avpqst', operator_left, operator_right, precision=lax.Precision.HIGHEST)
    return joined.reshape(channels, channels, 4, 4)

def reference(wavefunction, left_environment, operator_left, operator_right, right_environment, row_sector):
    combined = combine_operators(operator_left, operator_right)
    state_matrix = wavefunction.reshape(BOND_WIDTH, 4 * BOND_WIDTH)
    right_matrix = right_environment.reshape(CHANNELS * BOND_WIDTH, BOND_WIDTH)
    blocks = left_environment.reshape(CHANNELS, TILES, ROW_DEV, BOND_WIDTH).transpose(1, 0, 2, 3)

    def apply_block(left_block):
        left_part = jnp.dot(left_block.reshape(CHANNELS * ROW_DEV, BOND_WIDTH), state_matrix, preferred_element_type=jnp.float32)
        left_part = left_part.reshape(CHANNELS, ROW_DEV, 4, BOND_WIDTH)
        mixed_part = jnp.einsum('avyx,alxr->lyvr', combined, left_part, precision=lax.Precision.HIGHEST).astype(jnp.bfloat16)
        result = jnp.dot(mixed_part.reshape(ROW_DEV * 4, CHANNELS * BOND_WIDTH), right_matrix, preferred_element_type=jnp.float32)
        return result.astype(jnp.bfloat16).reshape(ROW_DEV, 4, BOND_WIDTH)
    applied = lax.map(apply_block, blocks).reshape(ROWS, 4, BOND_WIDTH)
    flat = applied.reshape(ROWS, 4 * BOND_WIDTH)
    gram = jnp.dot(flat, flat.T, preferred_element_type=jnp.float32)
    tile_labels = jnp.repeat(row_sector, ROW_DEV)
    same_sector = tile_labels[:, None] == tile_labels[None, :]
    density = jnp.where(same_sector, gram, jnp.float32(0.0)) * (1.0 / math.sqrt(4.0 * BOND_WIDTH))
    return (applied, density)
```

```python
import functools
import math

import jax
import jax.numpy as jnp
from jax import lax
from jax.experimental import pallas as pl
from jax.experimental.pallas import tpu as pltpu
from jax.sharding import PartitionSpec as P

BOND_WIDTH = 3072
ROW_BLOCKS = 4


def hop(value, mask):
    devices = lax.axis_size("lb")
    return lax.ppermute(value, "lb", [(i, i ^ mask) for i in range(devices)])


def rb_hop(value, mask):
    devices = lax.axis_size("rb")
    return lax.ppermute(value, "rb", [(i, i ^ mask) for i in range(devices)])


def spread(piece, bits):
    held = {0: piece}
    for bit in bits:
        held.update({q | bit: hop(held[q], 2 * bit) for q in list(held)})
    return held


def combine_operators(operator_left, operator_right):
    channels = operator_left.shape[0]
    joined = jnp.einsum(
        "aups,uvqt->avpqst", operator_left, operator_right, precision=lax.Precision.HIGHEST
    )
    return joined.reshape(channels, channels, 4, 4)


def right_kernel(chips, steps, own_ref, sib_ref, *refs):
    first, second = refs[:chips], refs[chips : 2 * chips]
    out_ref, total = refs[2 * chips :]
    step = pl.program_id(0)
    rows, width = own_ref.shape[0], first[0].shape[1]

    @pl.when(step == 0)
    def _():
        total[...] = jnp.zeros_like(total)

    def add(pieces):
        for e, lhs in enumerate((own_ref, sib_ref)):
            here = pl.ds(e * rows, rows)
            if width % 128 == 0:
                rhs = jnp.concatenate([p[...] for p in pieces], axis=1)
                value = jnp.dot(lhs[...], rhs, preferred_element_type=jnp.float32)
                for q in range(chips):
                    total[q, here, :] += value[:, q * width : (q + 1) * width]
            else:
                for q in range(chips):
                    total[q, here, :] += jnp.dot(
                        lhs[...], pieces[q][...], preferred_element_type=jnp.float32
                    )

    @pl.when(step < steps // 2)
    def _():
        add(first)

    @pl.when(step >= steps // 2)
    def _():
        add(second)

    @pl.when(step == steps - 1)
    def _():
        out_ref[...] = total[...].astype(out_ref.dtype)


def right_product(own, sib, first, second, steps):
    chips = len(first)
    rows, depth = own.shape
    width = first[0].shape[1]
    block = depth // steps
    half = steps // 2
    lhs_spec = pl.BlockSpec((rows, block), lambda k: (0, k))
    first_spec = pl.BlockSpec((block, width), lambda k: (jnp.minimum(k, half - 1), 0))
    second_spec = pl.BlockSpec((block, width), lambda k: (jnp.maximum(k - half, 0), 0))
    shape = (chips, 2 * rows, width)
    return pl.pallas_call(
        functools.partial(right_kernel, chips, steps),
        out_shape=jax.ShapeDtypeStruct(shape, jnp.bfloat16),
        grid=(steps,),
        in_specs=[lhs_spec] * 2 + [first_spec] * chips + [second_spec] * chips,
        out_specs=pl.BlockSpec(shape, lambda k: (0, 0, 0)),
        scratch_shapes=[pltpu.VMEM(shape, jnp.float32)],
        cost_estimate=pl.CostEstimate(
            flops=4 * rows * depth * chips * width,
            bytes_accessed=2 * depth * (2 * rows + chips * width),
            transcendentals=0,
        ),
        name="right_product",
    )(own, sib, *first, *second)


def exchange(parts, own_slot):
    devices = lax.axis_size("rb")
    z = lax.axis_index("rb")

    def slot(target):
        return lax.dynamic_index_in_dim(parts, target ^ own_slot, 0, keepdims=False)

    total = slot(z).astype(jnp.float32)
    for mask in range(1, devices):
        total = total + rb_hop(slot(z ^ mask), mask).astype(jnp.float32)
    return total


def shards(
    wavefunction, left_environment, operator_left, operator_right, right_environment, row_sector
):
    channels, row_count, full_bond = left_environment.shape
    piece_rows, states, local_right = wavefunction.shape
    tile_width = right_environment.shape[2]
    tiles = lax.axis_size("lb")
    chips = tiles // 2
    me = lax.axis_index("lb")
    z = lax.axis_index("rb")
    chip, core = me // 2, me % 2
    first_core = core == 0
    bits = [1 << i for i in range(chips.bit_length() - 1)]
    orders = (bits[::-1], bits)

    flat = wavefunction.reshape(piece_rows, states * local_right)
    half_rows = piece_rows // 2
    state = jnp.zeros((full_bond, states * local_right), wavefunction.dtype)
    for half in range(2):
        held = spread(flat[half * half_rows : (half + 1) * half_rows], orders[half])
        for q, piece in held.items():
            for e in range(2):
                value = piece if e == 0 else hop(piece, 1)
                start = (me ^ (2 * q + e)) * piece_rows + half * half_rows
                state = lax.dynamic_update_slice(state, value, (start, jnp.int32(0)))

    combined = combine_operators(operator_left, operator_right)
    block_rows = row_count // ROW_BLOCKS
    mixed = []
    for s in range(ROW_BLOCKS):
        rows = left_environment[:, s * block_rows : (s + 1) * block_rows]
        left_part = jnp.dot(
            rows.reshape(channels * block_rows, full_bond),
            state,
            preferred_element_type=jnp.float32,
        ).reshape(channels, block_rows, states, local_right)
        part = jnp.einsum(
            "avyx,alxr->lyvr", combined, left_part, precision=lax.Precision.HIGHEST
        ).astype(jnp.bfloat16)
        mixed.append(part.reshape(block_rows * states, channels * local_right))
    mixed = jnp.concatenate(mixed, axis=0)
    mixed_sibling = hop(mixed, 1)

    chunks = max(1, tile_width // 128)
    width = tile_width // chunks
    half = channels // 2
    mine, theirs = [], []
    gram = [0.0] * chips
    for j in range(chunks):
        columns = right_environment[:, :, j * width : (j + 1) * width]
        pieces = []
        for h in range(2):
            part = columns[h * half : (h + 1) * half].reshape(half * local_right, width)
            held = spread(part, orders[h])
            pieces.append([held[q] for q in range(chips)])
        parts = right_product(mixed, mixed_sibling, pieces[0], pieces[1], channels)
        applied = exchange(parts, chip).astype(jnp.bfloat16)
        own_rows = row_count * states
        mine.append(applied[:own_rows])
        theirs.append(hop(applied[own_rows:], 1))
        flat_tiles = applied.reshape(2 * row_count, states * width)
        others = spread(flat_tiles, orders[j % 2])
        for q in range(chips):
            gram[q] = gram[q] + lax.dot_general(
                flat_tiles,
                others[q],
                (((1,), (1,)), ((), ())),
                preferred_element_type=jnp.float32,
            )

    def ordered(value, other):
        return (jnp.where(first_core, value, other), jnp.where(first_core, other, value))

    columns = [ordered(a, b) for a, b in zip(mine, theirs)]
    applied = jnp.concatenate([c[0] for c in columns] + [c[1] for c in columns], axis=1)
    applied = applied.reshape(row_count, states, 2 * tile_width)

    gram = jnp.stack(gram)
    received = hop(gram[:, row_count:].astype(jnp.bfloat16), 1).astype(jnp.float32)
    kept = gram[:, :row_count]
    own_first = kept[:, :, :row_count] + received[:, :, row_count:]
    own_second = kept[:, :, row_count:] + received[:, :, :row_count]
    gram = jnp.concatenate(ordered(own_first, own_second), axis=2).astype(jnp.bfloat16)
    block = exchange(gram, chip)
    own_label = lax.dynamic_index_in_dim(row_sector, me, keepdims=False)
    labels = lax.dynamic_slice_in_dim(row_sector, 2 * z, 2)
    keep = jnp.repeat(labels == own_label, row_count)[None, :]
    density = jnp.where(keep, block, jnp.float32(0.0)) * (1.0 / math.sqrt(4.0 * BOND_WIDTH))
    return (applied, density)


def solution(mesh):
    placed = (P("lb", None, "rb"), P(None, "lb", None), P(), P(), P(None, "rb", "lb"), P())
    return jax.shard_map(
        shards,
        mesh=mesh,
        in_specs=placed,
        out_specs=(P("lb", None, "rb"), P("lb", "rb")),
        check_vma=False,
    )
```

```python
import functools
import math

import jax
import jax.numpy as jnp
from jax import lax
from jax.experimental import pallas as pl
from jax.experimental.pallas import tpu as pltpu
from jax.sharding import PartitionSpec as P


BOND_WIDTH = 3072
ROW_BLOCKS = 4


def hop(value, mask):
    devices = lax.axis_size("lb")
    return lax.ppermute(value, "lb", [(i, i ^ mask) for i in range(devices)])


def rb_hop(value, mask):
    devices = lax.axis_size("rb")
    return lax.ppermute(value, "rb", [(i, i ^ mask) for i in range(devices)])


def spread(piece, bits):
    held = {0: piece}
    for bit in bits:
        for q in list(held):
            held[q | bit] = hop(held[q], 2 * bit)
    return held


def combine_operators(operator_left, operator_right):
    channels = operator_left.shape[0]
    joined = jnp.einsum(
        "aups,uvqt->avpqst", operator_left, operator_right, precision=lax.Precision.HIGHEST
    )
    return joined.reshape(channels, channels, 4, 4)


def right_kernel(chips, blocks, steps, *refs):
    lhs, refs = refs[: 2 * blocks], refs[2 * blocks :]
    first, second = refs[:chips], refs[chips : 2 * chips]
    out_ref, rhs, total = refs[2 * chips :]
    step = pl.program_id(0)
    width = first[0].shape[1]

    @pl.when(step == 0)
    def _():
        total[...] = jnp.zeros_like(total)

    def load(pieces):
        for q in range(chips):
            rhs[:, q * width : (q + 1) * width] = pieces[q][...]

    @pl.when(step < steps // 2)
    def _():
        load(first)

    @pl.when(step >= steps // 2)
    def _():
        load(second)

    rows = blocks * lhs[0].shape[0]
    for e in range(2):
        left = jnp.concatenate([r[...] for r in lhs[e * blocks : (e + 1) * blocks]], axis=0)
        total[e * rows : (e + 1) * rows, :] += jnp.dot(
            left, rhs[...], preferred_element_type=jnp.float32
        )

    @pl.when(step == steps - 1)
    def _():
        for q in range(chips):
            out_ref[q] = total[:, q * width : (q + 1) * width].astype(out_ref.dtype)


def right_product(own, sib, first, second, steps):
    chips, blocks = len(first), len(own)
    block_rows, depth = own[0].shape
    rows = 2 * blocks * block_rows
    width = first[0].shape[1]
    block = depth // steps
    half = steps // 2
    lhs_spec = pl.BlockSpec((block_rows, block), lambda k: (0, k))
    first_spec = pl.BlockSpec((block, width), lambda k: (jnp.minimum(k, half - 1), 0))
    second_spec = pl.BlockSpec((block, width), lambda k: (jnp.maximum(k - half, 0), 0))
    shape = (chips, rows, width)
    return pl.pallas_call(
        functools.partial(right_kernel, chips, blocks, steps),
        out_shape=jax.ShapeDtypeStruct(shape, jnp.bfloat16),
        grid=(steps,),
        in_specs=[lhs_spec] * (2 * blocks) + [first_spec] * chips + [second_spec] * chips,
        out_specs=pl.BlockSpec(shape, lambda k: (0, 0, 0)),
        scratch_shapes=[
            pltpu.VMEM((block, chips * width), jnp.bfloat16),
            pltpu.VMEM((rows, chips * width), jnp.float32),
        ],
        cost_estimate=pl.CostEstimate(
            flops=2 * rows * depth * chips * width,
            bytes_accessed=2 * depth * (rows + chips * width),
            transcendentals=0,
        ),
        name="right_product",
    )(*own, *sib, *first, *second)


def exchange(parts, own_slot):
    devices = lax.axis_size("rb")
    z = lax.axis_index("rb")

    def slot(target):
        return lax.dynamic_index_in_dim(parts, target ^ own_slot, 0, keepdims=False)

    total = slot(z).astype(jnp.float32)
    for mask in range(1, devices):
        total = total + rb_hop(slot(z ^ mask), mask).astype(jnp.float32)
    return total


def shards(
    wavefunction, left_environment, operator_left, operator_right, right_environment, row_sector
):
    channels, row_count, full_bond = left_environment.shape
    piece_rows, states, local_right = wavefunction.shape
    tile_width = right_environment.shape[2]
    tiles = lax.axis_size("lb")
    chips = tiles // 2
    me = lax.axis_index("lb")
    z = lax.axis_index("rb")
    chip, core = me // 2, me % 2
    first_core = core == 0
    bits = [1 << i for i in range(chips.bit_length() - 1)]
    orders = (bits[::-1], bits)

    flat = wavefunction.reshape(piece_rows, states * local_right)
    half_rows = piece_rows // 2
    state = jnp.zeros((full_bond, states * local_right), wavefunction.dtype)
    for half in range(2):
        held = spread(flat[half * half_rows : (half + 1) * half_rows], orders[half])
        for q, piece in held.items():
            for e in range(2):
                value = piece if e == 0 else hop(piece, 1)
                start = (me ^ (2 * q + e)) * piece_rows + half * half_rows
                state = lax.dynamic_update_slice(state, value, (start, jnp.int32(0)))

    combined = combine_operators(operator_left, operator_right)
    block_rows = row_count // ROW_BLOCKS
    mixed, mixed_sibling = [], []
    for s in range(ROW_BLOCKS):
        rows = left_environment[:, s * block_rows : (s + 1) * block_rows]
        left_part = jnp.dot(
            rows.reshape(channels * block_rows, full_bond),
            state,
            preferred_element_type=jnp.float32,
        )
        left_part = left_part.reshape(channels, block_rows, states, local_right)
        part = jnp.einsum(
            "avyx,alxr->lyvr", combined, left_part, precision=lax.Precision.HIGHEST
        ).astype(jnp.bfloat16)
        part = part.reshape(block_rows * states, channels * local_right)
        mixed.append(part)
        mixed_sibling.append(hop(part, 1))

    chunks = max(1, tile_width // 128)
    width = tile_width // chunks
    half = channels // 2
    mine, theirs = [], []
    gram = [0.0] * chips
    for j in range(chunks):
        columns = right_environment[:, :, j * width : (j + 1) * width]
        pieces = []
        for h in range(2):
            part = columns[h * half : (h + 1) * half].reshape(half * local_right, width)
            held = spread(part, orders[h])
            pieces.append([held[q] for q in range(chips)])
        parts = right_product(mixed, mixed_sibling, pieces[0], pieces[1], channels)
        applied = exchange(parts, chip).astype(jnp.bfloat16)
        own_rows = row_count * states
        mine.append(applied[:own_rows])
        theirs.append(hop(applied[own_rows:], 1))
        flat_tiles = applied.reshape(2 * row_count, states * width)
        others = spread(flat_tiles, orders[j % 2])
        for q in range(chips):
            gram[q] = gram[q] + lax.dot_general(
                flat_tiles,
                others[q],
                (((1,), (1,)), ((), ())),
                preferred_element_type=jnp.float32,
            )

    def ordered(value, other):
        return (jnp.where(first_core, value, other), jnp.where(first_core, other, value))

    columns = [ordered(a, b) for a, b in zip(mine, theirs)]
    applied = jnp.concatenate([c[0] for c in columns] + [c[1] for c in columns], axis=1)
    applied = applied.reshape(row_count, states, 2 * tile_width)

    gram = jnp.stack(gram)
    received = hop(gram[:, row_count:].astype(jnp.bfloat16), 1).astype(jnp.float32)
    kept = gram[:, :row_count]
    own_first = kept[:, :, :row_count] + received[:, :, row_count:]
    own_second = kept[:, :, row_count:] + received[:, :, :row_count]
    gram = jnp.concatenate(ordered(own_first, own_second), axis=2).astype(jnp.bfloat16)
    block = exchange(gram, chip)
    own_label = lax.dynamic_index_in_dim(row_sector, me, keepdims=False)
    labels = lax.dynamic_slice_in_dim(row_sector, 2 * z, 2)
    keep = jnp.repeat(labels == own_label, row_count)[None, :]
    density = jnp.where(keep, block, jnp.float32(0.0)) * (1.0 / math.sqrt(4.0 * BOND_WIDTH))
    return (applied, density)


def solution(mesh):
    placed = (P("lb", None, "rb"), P(None, "lb", None), P(), P(), P(None, "rb", "lb"), P())
    return jax.shard_map(
        shards,
        mesh=mesh,
        in_specs=placed,
        out_specs=(P("lb", None, "rb"), P("lb", "rb")),
        check_vma=False,
    )
```

```python
import functools
import math

import jax
import jax.numpy as jnp
from jax import lax
from jax.experimental import pallas as pl
from jax.experimental.pallas import tpu as pltpu
from jax.sharding import PartitionSpec as P


BOND_WIDTH = 3072
ROW_BLOCKS = 2


def hop(value, mask):
    devices = lax.axis_size("lb")
    return lax.ppermute(value, "lb", [(i, i ^ mask) for i in range(devices)])


def rb_hop(value, mask):
    devices = lax.axis_size("rb")
    return lax.ppermute(value, "rb", [(i, i ^ mask) for i in range(devices)])


def spread(piece, bits):
    held = {0: piece}
    for bit in bits:
        for q in list(held):
            held[q | bit] = hop(held[q], 2 * bit)
    return held


def combine_operators(operator_left, operator_right):
    channels = operator_left.shape[0]
    joined = jnp.einsum(
        "aups,uvqt->avpqst", operator_left, operator_right, precision=lax.Precision.HIGHEST
    )
    return joined.reshape(channels, channels, 4, 4)


def right_kernel(chips, blocks, steps, *refs):
    lhs, refs = refs[: 2 * blocks], refs[2 * blocks :]
    first, second = refs[:chips], refs[chips : 2 * chips]
    out_ref, rhs, total = refs[2 * chips :]
    step = pl.program_id(0)
    width = first[0].shape[1]

    @pl.when(step == 0)
    def _():
        total[...] = jnp.zeros_like(total)

    def load(pieces):
        for q in range(chips):
            rhs[:, q * width : (q + 1) * width] = pieces[q][...]

    @pl.when(step < steps // 2)
    def _():
        load(first)

    @pl.when(step >= steps // 2)
    def _():
        load(second)

    rows = blocks * lhs[0].shape[0]
    for e in range(2):
        left = jnp.concatenate([r[...] for r in lhs[e * blocks : (e + 1) * blocks]], axis=0)
        total[e * rows : (e + 1) * rows, :] += jnp.dot(
            left, rhs[...], preferred_element_type=jnp.float32
        )

    @pl.when(step == steps - 1)
    def _():
        for q in range(chips):
            out_ref[q] = total[:, q * width : (q + 1) * width].astype(out_ref.dtype)


def right_product(own, sib, first, second, steps):
    chips, blocks = len(first), len(own)
    block_rows, depth = own[0].shape
    rows = 2 * blocks * block_rows
    width = first[0].shape[1]
    block = depth // steps
    half = steps // 2
    lhs_spec = pl.BlockSpec((block_rows, block), lambda k: (0, k))
    first_spec = pl.BlockSpec((block, width), lambda k: (jnp.minimum(k, half - 1), 0))
    second_spec = pl.BlockSpec((block, width), lambda k: (jnp.maximum(k - half, 0), 0))
    shape = (chips, rows, width)
    return pl.pallas_call(
        functools.partial(right_kernel, chips, blocks, steps),
        out_shape=jax.ShapeDtypeStruct(shape, jnp.bfloat16),
        grid=(steps,),
        in_specs=[lhs_spec] * (2 * blocks) + [first_spec] * chips + [second_spec] * chips,
        out_specs=pl.BlockSpec(shape, lambda k: (0, 0, 0)),
        scratch_shapes=[
            pltpu.VMEM((block, chips * width), jnp.bfloat16),
            pltpu.VMEM((rows, chips * width), jnp.float32),
        ],
        cost_estimate=pl.CostEstimate(
            flops=2 * rows * depth * chips * width,
            bytes_accessed=2 * depth * (rows + chips * width),
            transcendentals=0,
        ),
        name="right_product",
    )(*own, *sib, *first, *second)


def exchange(parts, own_slot):
    devices = lax.axis_size("rb")
    z = lax.axis_index("rb")

    def slot(target):
        return lax.dynamic_index_in_dim(parts, target ^ own_slot, 0, keepdims=False)

    total = slot(z).astype(jnp.float32)
    for mask in range(1, devices):
        total = total + rb_hop(slot(z ^ mask), mask).astype(jnp.float32)
    return total


def shards(
    wavefunction, left_environment, operator_left, operator_right, right_environment, row_sector
):
    channels, row_count, full_bond = left_environment.shape
    piece_rows, states, local_right = wavefunction.shape
    tile_width = right_environment.shape[2]
    tiles = lax.axis_size("lb")
    chips = tiles // 2
    me = lax.axis_index("lb")
    z = lax.axis_index("rb")
    chip, core = me // 2, me % 2
    first_core = core == 0
    bits = [1 << i for i in range(chips.bit_length() - 1)]
    orders = (bits[::-1], bits)

    flat = wavefunction.reshape(piece_rows, states * local_right)
    half_rows = piece_rows // 2
    state = jnp.zeros((full_bond, states * local_right), wavefunction.dtype)
    for half in range(2):
        held = spread(flat[half * half_rows : (half + 1) * half_rows], orders[half])
        for q, piece in held.items():
            for e in range(2):
                value = piece if e == 0 else hop(piece, 1)
                start = (me ^ (2 * q + e)) * piece_rows + half * half_rows
                state = lax.dynamic_update_slice(state, value, (start, jnp.int32(0)))

    combined = combine_operators(operator_left, operator_right).astype(jnp.bfloat16)
    block_rows = row_count // ROW_BLOCKS
    mixed, mixed_sibling = [], []
    for s in range(ROW_BLOCKS):
        rows = left_environment[:, s * block_rows : (s + 1) * block_rows]
        left_part = jnp.dot(
            rows.reshape(channels * block_rows, full_bond),
            state,
            preferred_element_type=jnp.float32,
        ).astype(jnp.bfloat16)
        left_part = left_part.reshape(channels, block_rows, states, local_right)
        part = jnp.einsum(
            "avyx,alxr->lyvr", combined, left_part, preferred_element_type=jnp.float32
        ).astype(jnp.bfloat16)
        part = part.reshape(block_rows * states, channels * local_right)
        mixed.append(part)
        mixed_sibling.append(hop(part, 1))

    chunks = max(1, tile_width // 128)
    width = tile_width // chunks
    half = channels // 2
    mine, theirs = [], []
    gram = [0.0] * chips
    for j in range(chunks):
        columns = right_environment[:, :, j * width : (j + 1) * width]
        pieces = []
        for h in range(2):
            part = columns[h * half : (h + 1) * half].reshape(half * local_right, width)
            held = spread(part, orders[h])
            pieces.append([held[q] for q in range(chips)])
        parts = right_product(mixed, mixed_sibling, pieces[0], pieces[1], channels)
        applied = exchange(parts, chip).astype(jnp.bfloat16)
        own_rows = row_count * states
        mine.append(applied[:own_rows])
        theirs.append(hop(applied[own_rows:], 1))
        flat_tiles = applied.reshape(2 * row_count, states * width)
        if j < chunks - 1:
            others = spread(flat_tiles, orders[j % 2])
        else:
            others = {q: hop(flat_tiles, 2 * q) if q else flat_tiles for q in range(chips)}
        for q in range(chips):
            gram[q] = gram[q] + lax.dot_general(
                flat_tiles,
                others[q],
                (((1,), (1,)), ((), ())),
                preferred_element_type=jnp.float32,
            )

    def ordered(value, other):
        return (jnp.where(first_core, value, other), jnp.where(first_core, other, value))

    columns = [ordered(a, b) for a, b in zip(mine, theirs)]
    applied = jnp.concatenate([c[0] for c in columns] + [c[1] for c in columns], axis=1)
    applied = applied.reshape(row_count, states, 2 * tile_width)

    gram = jnp.stack(gram)
    gram = jnp.concatenate(ordered(gram[:, :, :row_count], gram[:, :, row_count:]), axis=2)
    gram = gram.astype(jnp.bfloat16)
    rb_size = lax.axis_size("rb")
    block = 0.0
    for e in range(2):
        for mask in range(rb_size):
            part = lax.dynamic_index_in_dim(gram, (z ^ mask) ^ chip, 0, keepdims=False)
            part = part[e * row_count : (e + 1) * row_count]
            if e or mask:
                pairs = [
                    (b * rb_size + i, (b ^ e) * rb_size + (i ^ mask))
                    for b in range(tiles)
                    for i in range(rb_size)
                ]
                part = lax.ppermute(part, ("lb", "rb"), pairs)
            block = block + part.astype(jnp.float32)
    own_label = lax.dynamic_index_in_dim(row_sector, me, keepdims=False)
    labels = lax.dynamic_slice_in_dim(row_sector, 2 * z, 2)
    keep = jnp.repeat(labels == own_label, row_count)[None, :]
    density = jnp.where(keep, block, jnp.float32(0.0)) * (1.0 / math.sqrt(4.0 * BOND_WIDTH))
    return (applied, density)


def solution(mesh):
    placed = (P("lb", None, "rb"), P(None, "lb", None), P(), P(), P(None, "rb", "lb"), P())
    return jax.shard_map(
        shards,
        mesh=mesh,
        in_specs=placed,
        out_specs=(P("lb", None, "rb"), P("lb", "rb")),
        check_vma=False,
    )
```

```python
import functools
import math

import jax
import jax.numpy as jnp
from jax import lax
from jax.experimental import pallas as pl
from jax.experimental.pallas import tpu as pltpu
from jax.sharding import PartitionSpec as P


BOND_WIDTH = 3072
SECTOR_TILES = 4
GROUP = 8
CUTS = (0, 2, 4, 5, 6)
CHUNKS = len(CUTS) - 1


def hop(value, mask):
    devices = lax.axis_size("lb")
    return lax.ppermute(value, "lb", [(i, i ^ mask) for i in range(devices)])


def rb_hop(value, mask):
    devices = lax.axis_size("rb")
    return lax.ppermute(value, "rb", [(i, i ^ mask) for i in range(devices)])


def spread(piece, bits):
    held = {0: piece}
    for bit in bits:
        for q in list(held):
            held[q | bit] = hop(held[q], 2 * bit)
    return held


def combine_operators(operator_left, operator_right):
    channels = operator_left.shape[0]
    joined = jnp.einsum(
        "aups,uvqt->avpqst", operator_left, operator_right, precision=lax.Precision.HIGHEST
    )
    return joined.reshape(channels, channels, 4, 4)


def left_kernel(states, channels, group_rows, left_ref, mix_ref, *refs):
    waves, out_ref, parts = refs[:states], refs[states], refs[states + 1]
    for x in range(states):
        parts[x] = jnp.dot(
            left_ref[...], waves[x][...], preferred_element_type=jnp.float32
        ).astype(parts.dtype)
    rows = GROUP * channels
    for pair in range(group_rows // (2 * GROUP)):
        values = []
        for g in (2 * pair, 2 * pair + 1):
            stacked = jnp.concatenate(
                [parts[x, g * rows : (g + 1) * rows, :] for x in range(states)], axis=0
            )
            values.append(jnp.dot(mix_ref[...], stacked, preferred_element_type=jnp.float32))
        here = slice(2 * pair * GROUP, 2 * (pair + 1) * GROUP)
        for v in range(channels):
            for y in range(states):
                at = (v * states + y) * GROUP
                both = jnp.concatenate([value[at : at + GROUP] for value in values], axis=0)
                out_ref[v, y, here, :] = both.astype(out_ref.dtype)


def left_mix(left, mix, state, channels, states, group_rows):
    rows, depth = left.shape
    row_count = rows // channels
    local_right = state.shape[1] // states
    width = 256 if local_right % 256 == 0 else 128
    across = local_right // width
    wave_specs = [
        pl.BlockSpec((depth, width), lambda r, i, x=x: (0, x * across + r)) for x in range(states)
    ]
    return pl.pallas_call(
        functools.partial(left_kernel, states, channels, group_rows),
        out_shape=jax.ShapeDtypeStruct((channels, states, row_count, local_right), jnp.bfloat16),
        grid=(across, row_count // group_rows),
        in_specs=[
            pl.BlockSpec((group_rows * channels, depth), lambda r, i: (i, 0)),
            pl.BlockSpec(mix.shape, lambda r, i: (0, 0)),
            *wave_specs,
        ],
        out_specs=pl.BlockSpec((channels, states, group_rows, width), lambda r, i: (0, 0, i, r)),
        scratch_shapes=[pltpu.VMEM((states, group_rows * channels, width), jnp.bfloat16)],
        compiler_params=pltpu.CompilerParams(vmem_limit_bytes=60 << 20),
        cost_estimate=pl.CostEstimate(
            flops=2 * rows * depth * state.shape[1],
            bytes_accessed=2 * (depth * state.shape[1] + across * rows * depth),
            transcendentals=0,
        ),
        name="left_mix",
    )(left, mix, *([state] * states)).reshape(channels, states * row_count, local_right)


def right_kernel(chips, steps, per, own_ref, sib_ref, *refs):
    first, second = refs[:chips], refs[chips : 2 * chips]
    out_ref, rhs, total = refs[2 * chips :]
    step = pl.program_id(0)
    width = first[0].shape[0]
    rows = own_ref.shape[1]

    def load(pieces):
        for q in range(chips):
            rhs[q * width : (q + 1) * width, :] = pieces[q][...]

    pl.when(step < steps // 2)(lambda: load(first))
    pl.when(step >= steps // 2)(lambda: load(second))
    for e, ref in enumerate((own_ref, sib_ref)):
        here = slice(e * rows, (e + 1) * rows)
        left = jnp.concatenate([ref[v] for v in range(per)], axis=1)
        value = lax.dot_general(
            rhs[...], left, (((1,), (1,)), ((), ())), preferred_element_type=jnp.float32
        )

        @pl.when(step == 0)
        def _():
            total[:, here] = value

        @pl.when(jnp.logical_and(step > 0, step < steps - 1))
        def _():
            total[:, here] += value

        @pl.when(step == steps - 1)
        def _():
            final = (total[:, here] + value).astype(out_ref.dtype)
            for q in range(chips):
                out_ref[q, :, here] = final[q * width : (q + 1) * width]


def right_product(own, sib, first, second):
    chips = len(first)
    channels, rows, depth = own.shape
    width = first[0].shape[0]
    per = 2 if channels % 4 == 0 else 1
    steps = channels // per
    half = steps // 2
    lhs_spec = pl.BlockSpec((per, rows, depth), lambda k: (k, 0, 0))
    first_spec = pl.BlockSpec((width, per * depth), lambda k: (0, jnp.minimum(k, half - 1)))
    second_spec = pl.BlockSpec((width, per * depth), lambda k: (0, jnp.maximum(k - half, 0)))
    shape = (chips, width, 2 * rows)
    return pl.pallas_call(
        functools.partial(right_kernel, chips, steps, per),
        out_shape=jax.ShapeDtypeStruct(shape, jnp.bfloat16),
        grid=(steps,),
        in_specs=[lhs_spec] * 2 + [first_spec] * chips + [second_spec] * chips,
        out_specs=pl.BlockSpec(shape, lambda k: (0, 0, 0)),
        scratch_shapes=[
            pltpu.VMEM((chips * width, per * depth), jnp.bfloat16),
            pltpu.VMEM((chips * width, 2 * rows), jnp.float32),
        ],
        compiler_params=pltpu.CompilerParams(vmem_limit_bytes=60 << 20),
        cost_estimate=pl.CostEstimate(
            flops=4 * rows * depth * channels * chips * width,
            bytes_accessed=2 * depth * channels * (2 * rows + chips * width),
            transcendentals=0,
        ),
        name="right_product",
    )(own, sib, *first, *second)


def gram_kernel(chips, states, rows, start, *refs):
    tiles, out_ref = refs[:chips], refs[-1]

    def stacked(ref):
        parts = []
        for y in range(states):
            both = [ref[:, (e * states + y) * rows : (e * states + y + 1) * rows] for e in range(2)]
            parts.append(jnp.concatenate(both, axis=1))
        return jnp.concatenate(parts, axis=0)

    own = stacked(tiles[0])
    for q in range(chips):
        other = own if q == 0 else stacked(tiles[q])
        value = lax.dot_general(
            own, other, (((0,), (0,)), ((), ())), preferred_element_type=jnp.float32
        )
        out_ref[q] = value if start else refs[chips][q] + value


def add_gram(gram, tiles, states, rows):
    chips = len(tiles)
    shape = (chips, 2 * rows, 2 * rows)
    before = [] if gram is None else [gram]
    whole = pl.BlockSpec(memory_space=pltpu.VMEM)
    return pl.pallas_call(
        functools.partial(gram_kernel, chips, states, rows, gram is None),
        out_shape=jax.ShapeDtypeStruct(shape, jnp.float32),
        in_specs=[whole] * (chips + len(before)),
        out_specs=whole,
        compiler_params=pltpu.CompilerParams(vmem_limit_bytes=32 << 20),
        cost_estimate=pl.CostEstimate(
            flops=2 * chips * (2 * rows) ** 2 * states * tiles[0].shape[0],
            bytes_accessed=8 * chips * (2 * rows) ** 2,
            transcendentals=0,
        ),
        name="add_gram",
    )(*tiles, *before)


def exchange(parts, own_slot):
    z = lax.axis_index("rb")

    def slot(target):
        return lax.dynamic_index_in_dim(parts, target ^ own_slot, 0, keepdims=False)

    total = slot(z).astype(jnp.float32)
    for mask in range(1, lax.axis_size("rb")):
        total = total + rb_hop(slot(z ^ mask), mask).astype(jnp.float32)
    return total


def fetch(value, q):
    tiles = lax.axis_size("lb")
    near = [i for i in range(tiles) if 2 * abs(i // 2 - (i // 2 ^ q)) - 1 < SECTOR_TILES]
    return lax.ppermute(value, "lb", [(i ^ (2 * q), i) for i in near])


def shards(
    wavefunction, left_environment, operator_left, operator_right, right_environment, row_sector
):
    channels, row_count, full_bond = left_environment.shape
    piece_rows, states, local_right = wavefunction.shape
    tile_width = right_environment.shape[2]
    tiles = lax.axis_size("lb")
    chips = tiles // 2
    me = lax.axis_index("lb")
    z = lax.axis_index("rb")
    chip, core = me // 2, me % 2
    first_core = core == 0
    bits = [1 << i for i in range(chips.bit_length() - 1)]
    orders = (bits[::-1], bits)

    flat = wavefunction.reshape(piece_rows, states * local_right)
    half_rows = piece_rows // 2
    state = jnp.zeros((full_bond, states * local_right), wavefunction.dtype)
    for half in range(2):
        held = spread(flat[half * half_rows : (half + 1) * half_rows], orders[half])
        for q, piece in held.items():
            for e in range(2):
                value = piece if e == 0 else hop(piece, 1)
                start = (me ^ (2 * q + e)) * piece_rows + half * half_rows
                state = lax.dynamic_update_slice(state, value, (start, jnp.int32(0)))

    combined = combine_operators(operator_left, operator_right)
    mix = combined.transpose(1, 2, 3, 0)[:, :, None, :, None, :]
    mix = mix * jnp.eye(GROUP, dtype=jnp.float32)[None, None, :, None, :, None]
    mix = mix.reshape(channels * GROUP * states, states * GROUP * channels).astype(jnp.bfloat16)
    left = left_environment.transpose(1, 0, 2).reshape(row_count * channels, full_bond)
    mixed = left_mix(left, mix, state, channels, states, row_count // 2)
    mixed_sibling = hop(mixed, 1)

    half = channels // 2
    flipped = right_environment.transpose(2, 0, 1).reshape(tile_width, channels * local_right)
    mine, theirs = [], []
    gram = None
    for j in range(CHUNKS):
        here = slice(CUTS[j] * tile_width // CUTS[-1], CUTS[j + 1] * tile_width // CUTS[-1])
        pieces = []
        for h in range(2):
            part = flipped[here, h * half * local_right : (h + 1) * half * local_right]
            held = spread(part, orders[h])
            pieces.append([held[q] for q in range(chips)])
        parts = right_product(mixed, mixed_sibling, *pieces)
        applied = exchange(parts, chip).astype(jnp.bfloat16)
        own_rows = row_count * states
        mine.append(applied[:, :own_rows])
        theirs.append(hop(applied[:, own_rows:], 1))
        if j < CHUNKS // 2:
            held = spread(applied, orders[j % 2])
        else:
            held = {q: fetch(applied, q) if q else applied for q in range(chips)}
        gram = add_gram(gram, [held[q] for q in range(chips)], states, row_count)

    def ordered(value, other):
        return (jnp.where(first_core, value, other), jnp.where(first_core, other, value))

    gram = jnp.concatenate(ordered(gram[:, :, :row_count], gram[:, :, row_count:]), axis=2)
    gram = gram.astype(jnp.bfloat16)
    rb_size = lax.axis_size("rb")
    block = 0.0
    for e in range(2):
        for mask in range(rb_size):
            part = lax.dynamic_index_in_dim(gram, (z ^ mask) ^ chip, 0, keepdims=False)
            part = part[e * row_count : (e + 1) * row_count]
            if e or mask:
                pairs = [
                    (b * rb_size + i, (b ^ e) * rb_size + (i ^ mask))
                    for b in range(tiles)
                    for i in range(rb_size)
                ]
                part = lax.ppermute(part, ("lb", "rb"), pairs)
            block = block + part.astype(jnp.float32)
    columns = [ordered(a, b) for a, b in zip(mine, theirs)]
    applied = jnp.concatenate([c[0] for c in columns] + [c[1] for c in columns], axis=0)
    applied = applied.reshape(2 * tile_width, states, row_count).transpose(2, 1, 0)
    own_label = lax.dynamic_index_in_dim(row_sector, me, keepdims=False)
    labels = lax.dynamic_slice_in_dim(row_sector, 2 * z, 2)
    keep = jnp.repeat(labels == own_label, row_count)[None, :]
    density = jnp.where(keep, block, jnp.float32(0.0)) * (1.0 / math.sqrt(4.0 * BOND_WIDTH))
    return (applied, density)


def solution(mesh):
    placed = (P("lb", None, "rb"), P(None, "lb", None), P(), P(), P(None, "rb", "lb"), P())
    return jax.shard_map(
        shards,
        mesh=mesh,
        in_specs=placed,
        out_specs=(P("lb", None, "rb"), P("lb", "rb")),
        check_vma=False,
    )
```

```python
import functools
import math

import jax
import jax.numpy as jnp
from jax import lax
from jax.experimental import pallas as pl
from jax.experimental.pallas import tpu as pltpu
from jax.sharding import PartitionSpec as P


BOND_WIDTH = 3072
SECTOR_TILES = 4
GROUP = 8
CUTS = (0, 2, 4, 5, 6)
CHUNKS = len(CUTS) - 1


def hop(value, mask):
    devices = lax.axis_size("lb")
    return lax.ppermute(value, "lb", [(i, i ^ mask) for i in range(devices)])


def rb_hop(value, mask):
    devices = lax.axis_size("rb")
    return lax.ppermute(value, "rb", [(i, i ^ mask) for i in range(devices)])


def spread(piece, bits):
    held = {0: piece}
    for bit in bits:
        for q in list(held):
            held[q | bit] = hop(held[q], 2 * bit)
    return held


def combine_operators(operator_left, operator_right):
    channels = operator_left.shape[0]
    joined = jnp.einsum(
        "aups,uvqt->avpqst", operator_left, operator_right, precision=lax.Precision.HIGHEST
    )
    return joined.reshape(channels, channels, 4, 4)


def left_kernel(states, channels, group_rows, left_ref, mix_ref, *refs):
    waves, out_ref, parts = refs[:states], refs[states], refs[states + 1]
    for x in range(states):
        parts[x] = jnp.dot(
            left_ref[...], waves[x][...], preferred_element_type=jnp.float32
        ).astype(parts.dtype)
    rows = GROUP * channels
    for pair in range(group_rows // (2 * GROUP)):
        values = []
        for g in (2 * pair, 2 * pair + 1):
            stacked = jnp.concatenate(
                [parts[x, g * rows : (g + 1) * rows, :] for x in range(states)], axis=0
            )
            values.append(jnp.dot(mix_ref[...], stacked, preferred_element_type=jnp.float32))
        here = slice(2 * pair * GROUP, 2 * (pair + 1) * GROUP)
        for v in range(channels):
            for y in range(states):
                at = (v * states + y) * GROUP
                both = jnp.concatenate([value[at : at + GROUP] for value in values], axis=0)
                out_ref[v, y, here, :] = both.astype(out_ref.dtype)


def left_mix(left, mix, state, channels, states, group_rows):
    rows, depth = left.shape
    row_count = rows // channels
    local_right = state.shape[1] // states
    width = 256 if local_right % 256 == 0 else 128
    across = local_right // width
    wave_specs = [
        pl.BlockSpec((depth, width), lambda r, i, x=x: (0, x * across + r)) for x in range(states)
    ]
    return pl.pallas_call(
        functools.partial(left_kernel, states, channels, group_rows),
        out_shape=jax.ShapeDtypeStruct((channels, states, row_count, local_right), jnp.bfloat16),
        grid=(across, row_count // group_rows),
        in_specs=[
            pl.BlockSpec((group_rows * channels, depth), lambda r, i: (i, 0)),
            pl.BlockSpec(mix.shape, lambda r, i: (0, 0)),
            *wave_specs,
        ],
        out_specs=pl.BlockSpec((channels, states, group_rows, width), lambda r, i: (0, 0, i, r)),
        scratch_shapes=[pltpu.VMEM((states, group_rows * channels, width), jnp.bfloat16)],
        compiler_params=pltpu.CompilerParams(vmem_limit_bytes=60 << 20),
        cost_estimate=pl.CostEstimate(
            flops=2 * rows * depth * state.shape[1],
            bytes_accessed=2 * (depth * state.shape[1] + across * rows * depth),
            transcendentals=0,
        ),
        name="left_mix",
    )(left, mix, *([state] * states)).reshape(channels, states * row_count, local_right)


def right_kernel(chips, steps, per, turn_ref, own_ref, sib_ref, *refs):
    first, second = refs[:chips], refs[chips : 2 * chips]
    outs = refs[2 * chips : 3 * chips]
    rhs, total = refs[3 * chips :]
    step = pl.program_id(0)
    width = first[0].shape[0]
    rows = own_ref.shape[1]

    def load(pieces):
        for q in range(chips):
            rhs[q * width : (q + 1) * width, :] = pieces[q][...]

    pl.when(step < steps // 2)(lambda: load(first))
    pl.when(step >= steps // 2)(lambda: load(second))
    for e, ref in enumerate((own_ref, sib_ref)):
        here = slice(e * rows, (e + 1) * rows)
        left = jnp.concatenate([ref[v] for v in range(per)], axis=1)
        value = lax.dot_general(
            rhs[...], left, (((1,), (1,)), ((), ())), preferred_element_type=jnp.float32
        )

        @pl.when(step == 0)
        def _():
            total[:, here] = value

        @pl.when(step > 0)
        def _():
            total[:, here] += value

    @pl.when(step == steps - 1)
    def _():
        for m in range(chips):
            at = pl.multiple_of((turn_ref[0] ^ m) * width, 16)
            outs[m][...] = total[pl.ds(at, width), :].astype(outs[m].dtype)


def right_product(turn, own, sib, first, second):
    chips = len(first)
    channels, rows, depth = own.shape
    width = first[0].shape[0]
    per = 2 if channels % 4 == 0 else 1
    steps = channels // per
    half = steps // 2
    shape = (width, 2 * rows)
    return pl.pallas_call(
        functools.partial(right_kernel, chips, steps, per),
        out_shape=[jax.ShapeDtypeStruct(shape, jnp.bfloat16)] * chips,
        grid_spec=pltpu.PrefetchScalarGridSpec(
            num_scalar_prefetch=1,
            grid=(steps,),
            in_specs=[pl.BlockSpec((per, rows, depth), lambda k, t: (k, 0, 0))] * 2
            + [pl.BlockSpec((width, per * depth), lambda k, t: (0, jnp.minimum(k, half - 1)))]
            * chips
            + [pl.BlockSpec((width, per * depth), lambda k, t: (0, jnp.maximum(k - half, 0)))]
            * chips,
            out_specs=[pl.BlockSpec(shape, lambda k, t: (0, 0))] * chips,
            scratch_shapes=[
                pltpu.VMEM((chips * width, per * depth), jnp.bfloat16),
                pltpu.VMEM((chips * width, 2 * rows), jnp.float32),
            ],
        ),
        compiler_params=pltpu.CompilerParams(vmem_limit_bytes=60 << 20),
        cost_estimate=pl.CostEstimate(
            flops=4 * rows * depth * channels * chips * width,
            bytes_accessed=2 * depth * channels * (2 * rows + chips * width),
            transcendentals=0,
        ),
        name="right_product",
    )(turn, own, sib, *first, *second)


def gram_kernel(chips, states, rows, start, *refs):
    tiles, out_ref = refs[:chips], refs[-1]

    def stacked(ref):
        parts = []
        for y in range(states):
            both = [ref[:, (e * states + y) * rows : (e * states + y + 1) * rows] for e in range(2)]
            parts.append(jnp.concatenate(both, axis=1))
        return jnp.concatenate(parts, axis=0)

    own = stacked(tiles[0])
    for q in range(chips):
        other = own if q == 0 else stacked(tiles[q])
        value = lax.dot_general(
            own, other, (((0,), (0,)), ((), ())), preferred_element_type=jnp.float32
        )
        out_ref[q] = value if start else refs[chips][q] + value


def add_gram(gram, tiles, states, rows):
    chips = len(tiles)
    shape = (chips, 2 * rows, 2 * rows)
    before = [] if gram is None else [gram]
    whole = pl.BlockSpec(memory_space=pltpu.VMEM)
    return pl.pallas_call(
        functools.partial(gram_kernel, chips, states, rows, gram is None),
        out_shape=jax.ShapeDtypeStruct(shape, jnp.float32),
        in_specs=[whole] * (chips + len(before)),
        out_specs=whole,
        compiler_params=pltpu.CompilerParams(vmem_limit_bytes=32 << 20),
        cost_estimate=pl.CostEstimate(
            flops=2 * chips * (2 * rows) ** 2 * states * tiles[0].shape[0],
            bytes_accessed=8 * chips * (2 * rows) ** 2,
            transcendentals=0,
        ),
        name="add_gram",
    )(*tiles, *before)


def exchange(parts):
    total = parts[0].astype(jnp.float32)
    for m in range(1, len(parts)):
        total = total + rb_hop(parts[m], m).astype(jnp.float32)
    return total


def fetch(value, q):
    tiles = lax.axis_size("lb")
    near = [i for i in range(tiles) if 2 * abs(i // 2 - (i // 2 ^ q)) - 1 < SECTOR_TILES]
    return lax.ppermute(value, "lb", [(i ^ (2 * q), i) for i in near])


def shards(
    wavefunction, left_environment, operator_left, operator_right, right_environment, row_sector
):
    channels, row_count, full_bond = left_environment.shape
    piece_rows, states, local_right = wavefunction.shape
    tile_width = right_environment.shape[2]
    tiles = lax.axis_size("lb")
    chips = tiles // 2
    me = lax.axis_index("lb")
    z = lax.axis_index("rb")
    chip, core = me // 2, me % 2
    first_core = core == 0
    bits = [1 << i for i in range(chips.bit_length() - 1)]
    orders = (bits[::-1], bits)

    half_rows = piece_rows // 2
    state = jnp.zeros((full_bond, states * local_right), wavefunction.dtype)
    for half in range(2):
        source = wavefunction if half == 0 else lax.optimization_barrier(wavefunction)
        piece = source[half * half_rows : (half + 1) * half_rows]
        held = spread(piece.reshape(half_rows, states * local_right), orders[half])
        for q, piece in held.items():
            for e in range(2):
                value = piece if e == 0 else hop(piece, 1)
                start = (me ^ (2 * q + e)) * piece_rows + half * half_rows
                state = lax.dynamic_update_slice(state, value, (start, jnp.int32(0)))

    combined = combine_operators(operator_left, operator_right)
    mix = combined.transpose(1, 2, 3, 0)[:, :, None, :, None, :]
    mix = mix * jnp.eye(GROUP, dtype=jnp.float32)[None, None, :, None, :, None]
    mix = mix.reshape(channels * GROUP * states, states * GROUP * channels).astype(jnp.bfloat16)
    left = left_environment.transpose(1, 0, 2).reshape(row_count * channels, full_bond)
    mixed = left_mix(left, mix, state, channels, states, row_count // 2)
    mixed_sibling = hop(mixed, 1)

    half = channels // 2
    flipped = right_environment.transpose(2, 0, 1).reshape(tile_width, channels * local_right)
    turn = (chip ^ z).astype(jnp.int32).reshape(1)
    mine, theirs = [], []
    gram = None
    for j in range(CHUNKS):
        here = slice(CUTS[j] * tile_width // CUTS[-1], CUTS[j + 1] * tile_width // CUTS[-1])
        pieces = []
        for h in range(2):
            part = flipped[here, h * half * local_right : (h + 1) * half * local_right]
            held = spread(part, orders[h])
            pieces.append([held[q] for q in range(chips)])
        parts = right_product(turn, mixed, mixed_sibling, *pieces)
        applied = exchange(parts).astype(jnp.bfloat16)
        own_rows = row_count * states
        mine.append(applied[:, :own_rows])
        theirs.append(hop(applied[:, own_rows:], 1))
        if j < CHUNKS // 2:
            held = spread(applied, orders[j % 2])
        else:
            held = {0: applied}
            for q in range(chips - 1, 0, -1):
                held[q] = fetch(applied, q)
        gram = add_gram(gram, [held[q] for q in range(chips)], states, row_count)

    def ordered(value, other):
        return (jnp.where(first_core, value, other), jnp.where(first_core, other, value))

    gram = jnp.concatenate(ordered(gram[:, :, :row_count], gram[:, :, row_count:]), axis=2)
    received = hop(gram[:, row_count:].astype(jnp.bfloat16), 1)
    gram = (gram[:, :row_count] + received.astype(jnp.float32)).astype(jnp.bfloat16)
    blocks = [
        lax.dynamic_index_in_dim(gram, turn[0] ^ m, 0, keepdims=False) for m in range(chips)
    ]
    block = exchange(blocks)
    columns = [ordered(a, b) for a, b in zip(mine, theirs)]
    applied = jnp.concatenate([c[0] for c in columns] + [c[1] for c in columns], axis=0)
    applied = applied.reshape(2 * tile_width, states, row_count).transpose(2, 1, 0)
    own_label = lax.dynamic_index_in_dim(row_sector, me, keepdims=False)
    labels = lax.dynamic_slice_in_dim(row_sector, 2 * z, 2)
    keep = jnp.repeat(labels == own_label, row_count)[None, :]
    density = jnp.where(keep, block, jnp.float32(0.0)) * (1.0 / math.sqrt(4.0 * BOND_WIDTH))
    return (applied, density)


def solution(mesh):
    placed = (P("lb", None, "rb"), P(None, "lb", None), P(), P(), P(None, "rb", "lb"), P())
    return jax.shard_map(
        shards,
        mesh=mesh,
        in_specs=placed,
        out_specs=(P("lb", None, "rb"), P("lb", "rb")),
        check_vma=False,
    )
```

```python
import functools
import math

import jax
import jax.numpy as jnp
from jax import lax
from jax.experimental import pallas as pl
from jax.experimental.pallas import tpu as pltpu
from jax.sharding import PartitionSpec as P


BOND_WIDTH = 3072
SECTOR_TILES = 4
GROUP = 8
CUTS = (0, 2, 4, 5, 6)
CHUNKS = len(CUTS) - 1


def hop(value, mask):
    devices = lax.axis_size("lb")
    return lax.ppermute(value, "lb", [(i, i ^ mask) for i in range(devices)])


def rb_hop(value, mask):
    devices = lax.axis_size("rb")
    return lax.ppermute(value, "rb", [(i, i ^ mask) for i in range(devices)])


def spread(piece, bits):
    held = {0: piece}
    for bit in bits:
        for q in list(held):
            held[q | bit] = hop(held[q], 2 * bit)
    return held


def combine_operators(operator_left, operator_right):
    channels = operator_left.shape[0]
    joined = jnp.einsum(
        "aups,uvqt->avpqst", operator_left, operator_right, precision=lax.Precision.HIGHEST
    )
    return joined.reshape(channels, channels, 4, 4)


def left_kernel(states, channels, group_rows, left_ref, mix_ref, *refs):
    waves, out_ref, parts = refs[:states], refs[states], refs[states + 1]
    for x in range(states):
        parts[x] = jnp.dot(
            left_ref[...], waves[x][...], preferred_element_type=jnp.float32
        ).astype(parts.dtype)
    rows = GROUP * channels
    for pair in range(group_rows // (2 * GROUP)):
        values = []
        for g in (2 * pair, 2 * pair + 1):
            stacked = jnp.concatenate(
                [parts[x, g * rows : (g + 1) * rows, :] for x in range(states)], axis=0
            )
            values.append(jnp.dot(mix_ref[...], stacked, preferred_element_type=jnp.float32))
        here = slice(2 * pair * GROUP, 2 * (pair + 1) * GROUP)
        for v in range(channels):
            for y in range(states):
                at = (v * states + y) * GROUP
                both = jnp.concatenate([value[at : at + GROUP] for value in values], axis=0)
                out_ref[v, y, here, :] = both.astype(out_ref.dtype)


def left_mix(left, mix, state, channels, states, group_rows):
    rows, depth = left.shape
    row_count = rows // channels
    local_right = state.shape[1] // states
    width = 256 if local_right % 256 == 0 else 128
    across = local_right // width
    wave_specs = [
        pl.BlockSpec((depth, width), lambda r, i, x=x: (0, x * across + r)) for x in range(states)
    ]
    return pl.pallas_call(
        functools.partial(left_kernel, states, channels, group_rows),
        out_shape=jax.ShapeDtypeStruct((channels, states, row_count, local_right), jnp.bfloat16),
        grid=(across, row_count // group_rows),
        in_specs=[
            pl.BlockSpec((group_rows * channels, depth), lambda r, i: (i, 0)),
            pl.BlockSpec(mix.shape, lambda r, i: (0, 0)),
            *wave_specs,
        ],
        out_specs=pl.BlockSpec((channels, states, group_rows, width), lambda r, i: (0, 0, i, r)),
        scratch_shapes=[pltpu.VMEM((states, group_rows * channels, width), jnp.bfloat16)],
        compiler_params=pltpu.CompilerParams(vmem_limit_bytes=60 << 20),
        cost_estimate=pl.CostEstimate(
            flops=2 * rows * depth * state.shape[1],
            bytes_accessed=2 * (depth * state.shape[1] + across * rows * depth),
            transcendentals=0,
        ),
        name="left_mix",
    )(left, mix, *([state] * states)).reshape(channels, states * row_count, local_right)


def right_kernel(chips, steps, per, turn_ref, own_ref, sib_ref, *refs):
    first, second = refs[:chips], refs[chips : 2 * chips]
    outs = refs[2 * chips : 3 * chips]
    rhs, total = refs[3 * chips :]
    step = pl.program_id(0)
    width = first[0].shape[0]
    rows = own_ref.shape[1]

    def load(pieces):
        for q in range(chips):
            rhs[q * width : (q + 1) * width, :] = pieces[q][...]

    pl.when(step < steps // 2)(lambda: load(first))
    pl.when(step >= steps // 2)(lambda: load(second))
    for e, ref in enumerate((own_ref, sib_ref)):
        here = slice(e * rows, (e + 1) * rows)
        left = jnp.concatenate([ref[v] for v in range(per)], axis=1)
        value = lax.dot_general(
            rhs[...], left, (((1,), (1,)), ((), ())), preferred_element_type=jnp.float32
        )

        @pl.when(step == 0)
        def _():
            total[:, here] = value

        @pl.when(step > 0)
        def _():
            total[:, here] += value

    @pl.when(step == steps - 1)
    def _():
        for m in range(chips):
            at = pl.multiple_of((turn_ref[0] ^ m) * width, 16)
            outs[m][...] = total[pl.ds(at, width), :].astype(outs[m].dtype)


def right_product(turn, own, sib, first, second):
    chips = len(first)
    channels, rows, depth = own.shape
    width = first[0].shape[0]
    per = (2 if width % 128 == 0 else 4) if channels % 8 == 0 else 1
    steps = channels // per
    half = steps // 2
    shape = (width, 2 * rows)
    return pl.pallas_call(
        functools.partial(right_kernel, chips, steps, per),
        out_shape=[jax.ShapeDtypeStruct(shape, jnp.bfloat16)] * chips,
        grid_spec=pltpu.PrefetchScalarGridSpec(
            num_scalar_prefetch=1,
            grid=(steps,),
            in_specs=[pl.BlockSpec((per, rows, depth), lambda k, t: (k, 0, 0))] * 2
            + [pl.BlockSpec((width, per * depth), lambda k, t: (0, jnp.minimum(k, half - 1)))]
            * chips
            + [pl.BlockSpec((width, per * depth), lambda k, t: (0, jnp.maximum(k - half, 0)))]
            * chips,
            out_specs=[pl.BlockSpec(shape, lambda k, t: (0, 0))] * chips,
            scratch_shapes=[
                pltpu.VMEM((chips * width, per * depth), jnp.bfloat16),
                pltpu.VMEM((chips * width, 2 * rows), jnp.float32),
            ],
        ),
        compiler_params=pltpu.CompilerParams(vmem_limit_bytes=60 << 20),
        cost_estimate=pl.CostEstimate(
            flops=4 * rows * depth * channels * chips * width,
            bytes_accessed=2 * depth * channels * (2 * rows + chips * width),
            transcendentals=0,
        ),
        name="right_product",
    )(turn, own, sib, *first, *second)


def gram_kernel(chips, states, rows, start, *refs):
    tiles, out_ref = refs[:chips], refs[-1]

    def stacked(ref):
        parts = []
        for y in range(states):
            both = [ref[:, (e * states + y) * rows : (e * states + y + 1) * rows] for e in range(2)]
            parts.append(jnp.concatenate(both, axis=1))
        return jnp.concatenate(parts, axis=0)

    own = stacked(tiles[0])
    for q in range(chips):
        other = own if q == 0 else stacked(tiles[q])
        value = lax.dot_general(
            own, other, (((0,), (0,)), ((), ())), preferred_element_type=jnp.float32
        )
        out_ref[q] = value if start else refs[chips][q] + value


def add_gram(gram, tiles, states, rows):
    chips = len(tiles)
    shape = (chips, 2 * rows, 2 * rows)
    before = [] if gram is None else [gram]
    whole = pl.BlockSpec(memory_space=pltpu.VMEM)
    return pl.pallas_call(
        functools.partial(gram_kernel, chips, states, rows, gram is None),
        out_shape=jax.ShapeDtypeStruct(shape, jnp.float32),
        in_specs=[whole] * (chips + len(before)),
        out_specs=whole,
        compiler_params=pltpu.CompilerParams(vmem_limit_bytes=32 << 20),
        cost_estimate=pl.CostEstimate(
            flops=2 * chips * (2 * rows) ** 2 * states * tiles[0].shape[0],
            bytes_accessed=8 * chips * (2 * rows) ** 2,
            transcendentals=0,
        ),
        name="add_gram",
    )(*tiles, *before)


def exchange(parts):
    total = parts[0].astype(jnp.float32)
    for m in range(1, len(parts)):
        part = rb_hop(parts[m], m)
        total = total + part.astype(jnp.float32)
    return total


def fetch(value, q):
    tiles = lax.axis_size("lb")
    near = [i for i in range(tiles) if 2 * abs(i // 2 - (i // 2 ^ q)) - 1 < SECTOR_TILES]
    return lax.ppermute(value, "lb", [(i ^ (2 * q), i) for i in near])


def shards(
    wavefunction, left_environment, operator_left, operator_right, right_environment, row_sector
):
    channels, row_count, full_bond = left_environment.shape
    piece_rows, states, local_right = wavefunction.shape
    tile_width = right_environment.shape[2]
    tiles = lax.axis_size("lb")
    chips = tiles // 2
    me = lax.axis_index("lb")
    z = lax.axis_index("rb")
    chip, core = me // 2, me % 2
    first_core = core == 0
    bits = [1 << i for i in range(chips.bit_length() - 1)]
    orders = (bits[::-1], bits)

    half_rows = piece_rows // 2
    state = jnp.zeros((full_bond, states * local_right), wavefunction.dtype)
    for half in range(2):
        source = wavefunction if half == 0 else lax.optimization_barrier(wavefunction)
        piece = source[half * half_rows : (half + 1) * half_rows]
        held = spread(piece.reshape(half_rows, states * local_right), orders[half])
        for q, piece in held.items():
            for e in range(2):
                value = piece if e == 0 else hop(piece, 1)
                start = (me ^ (2 * q + e)) * piece_rows + half * half_rows
                state = lax.dynamic_update_slice(state, value, (start, jnp.int32(0)))

    combined = combine_operators(operator_left, operator_right)
    mix = combined.transpose(1, 2, 3, 0)[:, :, None, :, None, :]
    mix = mix * jnp.eye(GROUP, dtype=jnp.float32)[None, None, :, None, :, None]
    mix = mix.reshape(channels * GROUP * states, states * GROUP * channels).astype(jnp.bfloat16)
    left = left_environment.transpose(1, 0, 2).reshape(row_count * channels, full_bond)
    mixed = left_mix(left, mix, state, channels, states, row_count // 2)
    mixed_sibling = hop(mixed, 1)

    half = channels // 2
    flipped = right_environment.transpose(2, 0, 1).reshape(tile_width, channels * local_right)
    turn = (chip ^ z).astype(jnp.int32).reshape(1)
    applied_parts = []
    gram = None
    for j in range(CHUNKS):
        here = slice(CUTS[j] * tile_width // CUTS[-1], CUTS[j + 1] * tile_width // CUTS[-1])
        pieces = []
        for h in range(2):
            part = flipped[here, h * half * local_right : (h + 1) * half * local_right]
            held = spread(part, orders[h])
            pieces.append([held[q] for q in range(chips)])
        parts = right_product(turn, mixed, mixed_sibling, *pieces)
        applied = exchange(parts).astype(jnp.bfloat16)
        applied_parts.append(applied)
        if j < CHUNKS // 2:
            held = spread(applied, orders[j % 2])
        else:
            held = {0: applied}
            for q in range(chips - 1, 0, -1):
                held[q] = fetch(applied, q)
        gram = add_gram(gram, [held[q] for q in range(chips)], states, row_count)

    def ordered(value, other):
        return (jnp.where(first_core, value, other), jnp.where(first_core, other, value))

    own_rows = row_count * states
    theirs = jnp.concatenate([part[:, own_rows:] for part in applied_parts], axis=0)
    theirs = hop(theirs, 1)

    gram = jnp.concatenate(ordered(gram[:, :, :row_count], gram[:, :, row_count:]), axis=2)
    received = hop(gram[:, row_count:].astype(jnp.bfloat16), 1)
    gram = (gram[:, :row_count] + received.astype(jnp.float32)).astype(jnp.bfloat16)
    blocks = [
        lax.dynamic_index_in_dim(gram, turn[0] ^ m, 0, keepdims=False) for m in range(chips)
    ]
    block = exchange(blocks)
    mine = jnp.concatenate([part[:, :own_rows] for part in applied_parts], axis=0)
    applied = jnp.concatenate(ordered(mine, theirs), axis=0)
    applied = applied.reshape(2 * tile_width, states, row_count).transpose(2, 1, 0)
    own_label = lax.dynamic_index_in_dim(row_sector, me, keepdims=False)
    labels = lax.dynamic_slice_in_dim(row_sector, 2 * z, 2)
    keep = jnp.repeat(labels == own_label, row_count)[None, :]
    density = jnp.where(keep, block, jnp.float32(0.0)) * (1.0 / math.sqrt(4.0 * BOND_WIDTH))
    return (applied, density)


def solution(mesh):
    placed = (P("lb", None, "rb"), P(None, "lb", None), P(), P(), P(None, "rb", "lb"), P())
    return jax.shard_map(
        shards,
        mesh=mesh,
        in_specs=placed,
        out_specs=(P("lb", None, "rb"), P("lb", "rb")),
        check_vma=False,
    )
```
